32 devices in a mesh: grp: 2 (over y), brick: 16 (over z, x, core).
Axes of the slice: x: 2, y: 2, z: 4, core: 2. Of those that a mesh axis runs over, the one named last changes fastest.
Arguments:
- low_factor: float32 [64, 16, 32, 512], P('brick', None, None, 'grp'), may hold values from -70 to 70, as said below
- test_matrix: float32 [512, 256], P('grp'), may hold values from -0.25 to 0.25
Outputs:
- basis: float32 [64, 16, 32, 256], P('brick')
- projected: float32 [256, 512], P(None, 'grp')
The draws below stay inside these ranges and needn't reach their ends.
Inputs may be any that keep to these rules, and one draw needn't show every extreme that they name: `low_factor`: A dense real factor.
All inputs are finite; a program needn't handle non-finite values.
Results may differ from the reference program's by a relative error of at most 0.0003.
Values sent between devices are 32-bit elements; how exact they have to be, the bound alone decides.
A program may use at most 64 MiB of HBM per device.

```python
import jax
import jax.numpy as jnp
from jax import lax

NY = 16
NZ = 32
GCOL = 256
RANK = 256
K = 512
NX = 64
N_GRP = 2


def draw_low_factor(key, part):
    keys = jax.random.split(jax.random.fold_in(key, 11), 3)
    shape = (NX, NY, NZ, K)
    values = jnp.clip(jax.random.normal(keys[0], shape, jnp.float32), -6.0, 6.0)
    position = jnp.arange(NX, dtype=jnp.float32) / jnp.float32(max(NX - 1, 1))
    rising = jnp.exp(jnp.log(3.0) * position)[:, None, None, None]
    cell_scale = jnp.exp(jax.random.uniform(keys[1], (NX, NY, NZ, 1), jnp.float32) * jnp.log(3.4))
    column_scale = jnp.exp(jax.random.uniform(keys[2], (1, 1, 1, K), jnp.float32) * jnp.log(10.0))
    scaled = values * rising * cell_scale * column_scale / 3.0
    return jnp.clip(scaled, -70.0, 70.0).astype(jnp.float32)


def block_levels(stream_key, shape, cuts, low, top_value):
    def one(dim, shards_of):
        steps = jax.random.uniform(jax.random.fold_in(jax.random.fold_in(stream_key, 6), dim), (shards_of,), jnp.float32, low / len(cuts), top_value / len(cuts))
        return jnp.repeat(jnp.exp(steps), shape[dim] // shards_of).reshape((-1,) + (1,) * (len(shape) - dim - 1))

    gain = one(*cuts[0])
    for cut in cuts[1:]:
        gain = gain * one(*cut)
    return gain


def normal_values(key, extent, width, limit, shards=(), held_as=jnp.bfloat16):
    values = jax.random.normal(key, extent, jnp.float32) * width
    if len(shards) > 0:
        values = block_levels(key, extent, shards, -0.22, 0.18) * values
    return jnp.clip(values, min=-limit, max=limit).astype(held_as)


def setup_inputs(seed: int = 0) -> dict:
    key_list = jax.random.split(jax.random.key(seed), 3)
    return {
        "low_factor": draw_low_factor(jax.random.fold_in(key_list[2], 71), 0),
        "test_matrix": normal_values(key_list[1], (K, RANK), K ** -0.5, 0.25, ((0, 2),), jnp.float32),
    }


DIFF = 0.12
CONV = 0.08
HIGH = lax.Precision.HIGHEST

def operate(field):
    padded = jnp.pad(field, ((1, 1), (1, 1), (1, 1), (0, 0)))
    xminus = padded[:-2, 1:-1, 1:-1]
    xplus = padded[2:, 1:-1, 1:-1]
    beside_all = xminus + xplus + padded[1:-1, :-2, 1:-1] + padded[1:-1, 2:, 1:-1]
    beside_all = beside_all + padded[1:-1, 1:-1, :-2] + padded[1:-1, 1:-1, 2:]
    return field - DIFF * beside_all - CONV * (xminus - xplus)

def reference(low_factor, test_matrix):
    cells = NX * NY * NZ

    def grown_group(group):
        start = (group * GCOL).astype(jnp.int32)
        piece = lax.dynamic_slice_in_dim(low_factor, start, GCOL, 3)
        return operate(operate(piece)).reshape(cells, GCOL)

    def add_group(group, total):
        start = (group * GCOL).astype(jnp.int32)
        omega = lax.dynamic_slice_in_dim(test_matrix, start, GCOL, 0)
        return total + jnp.dot(grown_group(group).astype(jnp.float32), omega.astype(jnp.float32), precision=HIGH, preferred_element_type=jnp.float32)
    sketch = lax.fori_loop(jnp.int32(0), jnp.int32(N_GRP), add_group, jnp.zeros((cells, RANK), jnp.float32))
    gram = lax.dot_general(sketch, sketch, (((0,), (0,)), ((), ())), precision=HIGH)
    lower = jnp.linalg.cholesky(gram)
    orthonormal = lax.linalg.triangular_solve(lower, sketch, left_side=False, lower=True, transpose_a=True)

    def project_group(group):
        return lax.dot_general(orthonormal, grown_group(group), (((0,), (0,)), ((), ())), precision=HIGH)
    blocks = lax.map(project_group, jnp.arange(N_GRP, dtype=jnp.int32))
    projected = jnp.moveaxis(blocks, 0, 1).reshape(RANK, K)
    basis = (orthonormal * jnp.sqrt(jnp.float32(cells))).reshape(NX, NY, NZ, RANK)
    return (basis, projected)
```

```python
import functools

import jax
import jax.numpy as jnp
from jax import lax
from jax.experimental import pallas as pl
from jax.experimental.pallas import tpu as pltpu
from jax.sharding import PartitionSpec as P

DIFF = 0.12
CONV = 0.08
HIGH = lax.Precision.HIGHEST
MESH = pl.DeviceIdType.MESH
BLOCK = 32


def dot(left, right, dims):
    return lax.dot_general(
        left, right, (dims, ((), ())), precision=HIGH, preferred_element_type=jnp.float32
    )


def chunk_ends(span_y, slab_x, groups):
    count = 4
    size = span_y // count
    if span_y % count or size < 3 or (slab_x * size) % groups or (slab_x * 2) % groups:
        return [(span_y, span_y, span_y)]
    ends = []
    for k in range(count):
        end = size * (k + 1)
        ends.append((end, end - 1, end - 2) if k < count - 1 else (end, end, end))
    return ends


def kernel(
    dims, x_hbm, omega, basis, projected,
    ext, first, grown, part, sketch, group_rx, gram, gram_rx, full, proj, proj_rx, proj_full, both,
    local_sem, halo_send, halo_recv, part_send, part_recv, back_send, back_recv, reduce_sem, gather_sem,
):
    groups, bricks, slab, span_y, span_z, cells = dims
    rank = omega.shape[1]
    cols = omega.shape[0]
    devices = groups * bricks
    me_g = lax.axis_index("grp")
    me_b = lax.axis_index("brick")
    me = me_g * bricks + me_b
    owners = min(bricks, rank // 8)
    strip = rank // owners
    ends = chunk_ends(span_y, slab, groups)

    def device(g, b):
        return {"grp": g, "brick": b}

    barrier = pltpu.get_barrier_semaphore()

    def greet(d, carry):
        other = lax.rem(me + d, devices)
        g = other // bricks
        pl.semaphore_signal(
            barrier, inc=1, device_id=device(g, other - g * bricks), device_id_type=MESH
        )
        return carry

    lax.fori_loop(1, devices, greet, 0)
    mine = pltpu.make_async_copy(
        x_hbm, ext.at[pl.ds(2, slab), pl.ds(1, span_y)], local_sem
    )
    mine.start()
    layer = (span_z, cols)
    for y in (0, span_y + 1):
        ext[:, y] = jnp.zeros((slab + 4,) + layer, jnp.float32)
        first[:, y] = jnp.zeros((slab + 2,) + layer, jnp.float32)

    @pl.when(me_b == 0)
    def _():
        ext[0:2] = jnp.zeros((2, span_y + 2) + layer, jnp.float32)

    @pl.when(me_b == bricks - 1)
    def _():
        ext[slab + 2 :] = jnp.zeros((2, span_y + 2) + layer, jnp.float32)

    pl.semaphore_wait(barrier, devices - 1)

    def halo(k, up):
        start = 0 if k == 0 else ends[k - 1][0]
        rows = ends[k][0] - start
        side = 0 if up else 1
        return pltpu.make_async_remote_copy(
            src_ref=x_hbm.at[pl.ds(slab - 2 if up else 0, 2), pl.ds(start, rows)],
            dst_ref=ext.at[pl.ds(0 if up else slab + 2, 2), pl.ds(1 + start, rows)],
            send_sem=halo_send.at[side, k],
            recv_sem=halo_recv.at[side, k],
            device_id=device(me_g, me_b + 1 if up else me_b - 1),
            device_id_type=MESH,
        )

    for k in range(len(ends)):
        @pl.when(me_b < bricks - 1)
        def _():
            halo(k, True).start()

        @pl.when(me_b > 0)
        def _():
            halo(k, False).start()

    mine.wait()

    def operate(mid, low, high, before, after):
        z = lax.broadcasted_iota(jnp.int32, mid.shape, mid.ndim - 2)
        down = jnp.where(z == 0, 0.0, pltpu.roll(mid, 1, mid.ndim - 2))
        up = jnp.where(z == span_z - 1, 0.0, pltpu.roll(mid, span_z - 1, mid.ndim - 2))
        beside = low + high + before + after + down + up
        return mid - DIFF * beside - CONV * (low - high)

    gate_low = jnp.where(me_b == 0, 0.0, 1.0)
    gate_high = jnp.where(me_b == bricks - 1, 0.0, 1.0)

    def first_row(y, carry):
        for i in range(slab + 2):
            value = operate(
                ext[i + 1, y + 1], ext[i, y + 1], ext[i + 2, y + 1], ext[i + 1, y], ext[i + 1, y + 2]
            )
            if i == 0:
                value = value * gate_low
            if i == slab + 1:
                value = value * gate_high
            first[i, y + 1] = value
        return carry

    def second_row(y, carry):
        values = []
        for i in range(slab):
            value = operate(
                first[i + 1, y + 1], first[i, y + 1], first[i + 2, y + 1],
                first[i + 1, y], first[i + 1, y + 2],
            )
            grown[y * slab + i] = value
            values.append(value)
        rows = jnp.concatenate(values, axis=0)
        terms = dot(rows, omega[...], ((1,), (0,)))
        part[pl.ds(y * slab, slab)] = terms.reshape(slab, span_z, rank)
        return carry

    def piece(k):
        start = 0 if k == 0 else ends[k - 1][2]
        pairs = (ends[k][2] - start) * slab // groups
        return start * slab, pairs

    def part_copy(k, d):
        start, pairs = piece(k)
        other = lax.rem(me_g + d, groups)
        return pltpu.make_async_remote_copy(
            src_ref=part.at[pl.ds(start + other * pairs, pairs)],
            dst_ref=group_rx.at[d - 1, pl.ds(start // groups, pairs)],
            send_sem=part_send.at[k, d - 1],
            recv_sem=part_recv.at[k, d - 1],
            device_id=device(other, me_b),
            device_id_type=MESH,
        )

    def back_copy(k, d):
        start, pairs = piece(k)
        other = lax.rem(me_g + d, groups)
        here = sketch.at[pl.ds(start + me_g * pairs, pairs)]
        return pltpu.make_async_remote_copy(
            src_ref=here,
            dst_ref=here,
            send_sem=back_send.at[k, d - 1],
            recv_sem=back_recv.at[k, d - 1],
            device_id=device(other, me_b),
            device_id_type=MESH,
        )

    def own_rows(k):
        start, pairs = piece(k)
        for d in range(1, groups):
            part_copy(k, d).wait_recv()

        def body(i, carry):
            at = start + me_g * pairs + i
            total = part[at]
            for d in range(groups - 1):
                total = total + group_rx[d, start // groups + i]
            sketch[at] = total
            return carry

        lax.fori_loop(0, pairs, body, 0)
        value = sketch[pl.ds(start + me_g * pairs, pairs)].reshape(pairs * span_z, rank)
        term = dot(value, value, ((0,), (0,)))
        if k == 0:
            gram[...] = term
        else:
            gram[...] += term

    for k, (end, end_first, end_second) in enumerate(ends):
        @pl.when(me_b > 0)
        def _():
            halo(k, True).wait_recv()

        @pl.when(me_b < bricks - 1)
        def _():
            halo(k, False).wait_recv()

        begin_first, begin_second = (0, 0) if k == 0 else ends[k - 1][1:]
        lax.fori_loop(begin_first, end_first, first_row, 0)
        lax.fori_loop(begin_second, end_second, second_row, 0)
        for d in range(1, groups):
            part_copy(k, d).start()
        if k > 0:
            own_rows(k - 1)
    own_rows(len(ends) - 1)

    def strip_at(o):
        return pl.ds(pl.multiple_of(o * strip, 8), strip)

    def to_owner(source, sink, sem, d, count, slot):
        other = lax.rem(me + d, devices) if count == devices else lax.rem(me_b + d, bricks)
        g = other // bricks if count == devices else me_g
        o = other - g * bricks if count == devices else other
        return o, pltpu.make_async_remote_copy(
            src_ref=source.at[strip_at(o)],
            dst_ref=sink.at[slot],
            send_sem=reduce_sem.at[sem, 0],
            recv_sem=reduce_sem.at[sem, 1],
            device_id=device(g, o),
            device_id_type=MESH,
        )

    def guarded(o, action):
        if owners == bricks:
            action()
        else:
            pl.when(o < owners)(action)

    def scatter_start(source, sink, sem, count, slot):
        def body(d, carry):
            def send():
                to_owner(source, sink, sem, d, count, slot)[1].start()

            o = lax.rem(me + d, bricks) if count == devices else lax.rem(me_b + d, bricks)
            guarded(o, send)
            return carry

        lax.fori_loop(1, count, body, 0)

        def keep():
            sink[slot] = source[strip_at(me_b)]

        guarded(me_b, keep)

    def bytes_wait(ref, sem):
        pltpu.make_async_copy(ref, ref, sem).wait()

    def scatter_finish(source, sink, sem, count, result):
        def receive():
            bytes_wait(sink.at[pl.ds(0, count - 1)], reduce_sem.at[sem, 1])

            def add(i, total):
                return total + sink[i]

            result[strip_at(me_b)] = lax.fori_loop(1, count, add, sink[0])

        guarded(me_b, receive)
        copies = count // bricks * owners
        if owners == bricks:
            bytes_wait(sink.at[pl.ds(0, copies - 1)], reduce_sem.at[sem, 0])
        else:
            @pl.when(me_b < owners)
            def _():
                bytes_wait(sink.at[pl.ds(0, copies - 1)], reduce_sem.at[sem, 0])

            @pl.when(me_b >= owners)
            def _():
                bytes_wait(sink.at[pl.ds(0, copies)], reduce_sem.at[sem, 0])

    def gather_start(result, sem):
        def body(d, carry):
            here = result.at[strip_at(me_b)]
            pltpu.make_async_remote_copy(
                src_ref=here,
                dst_ref=here,
                send_sem=gather_sem.at[sem, 0],
                recv_sem=gather_sem.at[sem, 1],
                device_id=device(me_g, lax.rem(me_b + d, bricks)),
                device_id_type=MESH,
            ).start()
            return carry

        def send():
            lax.fori_loop(1, bricks, body, 0)

        guarded(me_b, send)

    def gather_finish(result, sem, sink):
        rows = strip * (owners - 1)
        if owners == bricks:
            bytes_wait(result.at[pl.ds(0, rows)], gather_sem.at[sem, 1])
            bytes_wait(result.at[pl.ds(0, rows)], gather_sem.at[sem, 0])
        else:
            @pl.when(me_b < owners)
            def _():
                bytes_wait(result.at[pl.ds(0, rows)], gather_sem.at[sem, 1])
                bytes_wait(sink.at[pl.ds(0, bricks - 1)], gather_sem.at[sem, 0])

            @pl.when(me_b >= owners)
            def _():
                bytes_wait(result.at[...], gather_sem.at[sem, 1])

    scatter_start(gram, gram_rx, 0, devices, me)
    for k in range(len(ends)):
        for d in range(1, groups):
            back_copy(k, d).start()
    scatter_finish(gram, gram_rx, 0, devices, full)
    gather_start(full, 0)
    gather_finish(full, 0, gram_rx)

    both[:, 0:rank] = full[...]
    row = lax.broadcasted_iota(jnp.int32, (rank, rank), 0)
    col = lax.broadcasted_iota(jnp.int32, (rank, rank), 1)
    both[:, rank:] = jnp.where(row == col, 1.0, 0.0)

    def project():
        for k in range(len(ends)):
            for d in range(1, groups):
                back_copy(k, d).wait_recv()
        proj[...] = jnp.zeros_like(proj)

        @pl.loop(0, span_y)
        def _(y):
            left = sketch[pl.ds(y * slab, slab)].reshape(slab * span_z, rank)
            right = grown[pl.ds(y * slab, slab)].reshape(slab * span_z, cols)
            proj[...] += dot(left, right, ((0,), (0,)))

        scatter_start(proj, proj_rx, 1, bricks, me_b)

    def project_gather():
        scatter_finish(proj, proj_rx, 1, bricks, proj_full)
        gather_start(proj_full, 1)

    blocks = rank // BLOCK
    for block in range(blocks):
        if block == blocks // 2:
            project()
        if block == blocks - 1:
            project_gather()
        at = block * BLOCK
        panel = both[at : at + BLOCK, :]
        row = lax.broadcasted_iota(jnp.int32, (BLOCK, 1), 0)
        for j in range(BLOCK):
            pivot = panel[j : j + 1, :]
            scaled = pivot * (1.0 / pivot[:, at + j : at + j + 1])
            factor = jnp.where(row > j, panel[:, at + j : at + j + 1], 0.0)
            panel = panel - factor * scaled
        lane = lax.broadcasted_iota(jnp.int32, panel.shape, 1)
        full_row = lax.broadcasted_iota(jnp.int32, panel.shape, 0)
        diagonal = jnp.sum(
            jnp.where(lane == full_row + at, panel, 0.0), axis=1, keepdims=True
        )
        panel = panel * lax.rsqrt(diagonal)
        both[at : at + BLOCK, :] = panel
        if block < blocks - 1:
            below = dot(panel[:, 0:rank], panel, ((0,), (0,)))
            both[at + BLOCK :, :] = both[at + BLOCK :, :] - below[at + BLOCK :, :]

    inverse = both[:, rank:]
    scaled_inverse = inverse.T * jnp.sqrt(jnp.float32(cells))
    both[:, 0:rank] = scaled_inverse

    @pl.loop(0, span_y)
    def _(y):
        left = sketch[pl.ds(y * slab, slab)].reshape(slab * span_z, rank)
        value = dot(left, both[:, 0:rank], ((1,), (0,)))
        basis[:, y] = value.reshape(slab, span_z, rank)

    gather_finish(proj_full, 1, proj_rx)
    projected[...] = dot(both[:, rank:], proj_full[...], ((1,), (0,)))

    for k in range(len(ends)):
        @pl.when(me_b < bricks - 1)
        def _():
            halo(k, True).wait_send()

        @pl.when(me_b > 0)
        def _():
            halo(k, False).wait_send()

        for d in range(1, groups):
            part_copy(k, d).wait_send()
            back_copy(k, d).wait_send()


def shards(groups, bricks, low_factor, test_matrix):
    slab, span_y, span_z, cols = low_factor.shape
    rank = test_matrix.shape[1]
    pairs = slab * span_y
    cells = bricks * pairs * span_z
    owners = min(bricks, rank // 8)
    strip = rank // owners
    count = len(chunk_ends(span_y, slab, groups))
    vmem = lambda *shape: pltpu.VMEM(shape, jnp.float32)
    dma = pltpu.SemaphoreType.DMA
    return pl.pallas_call(
        functools.partial(kernel, (groups, bricks, slab, span_y, span_z, cells)),
        out_shape=(
            jax.ShapeDtypeStruct((slab, span_y, span_z, rank), jnp.float32),
            jax.ShapeDtypeStruct((rank, cols), jnp.float32),
        ),
        in_specs=[pl.BlockSpec(memory_space=pl.ANY), pl.BlockSpec(memory_space=pltpu.VMEM)],
        out_specs=[pl.BlockSpec(memory_space=pltpu.VMEM)] * 2,
        scratch_shapes=[
            vmem(slab + 4, span_y + 2, span_z, cols),
            vmem(slab + 2, span_y + 2, span_z, cols),
            vmem(pairs, span_z, cols),
            vmem(pairs, span_z, rank),
            vmem(pairs, span_z, rank),
            vmem(groups - 1, pairs // groups, span_z, rank),
            vmem(rank, rank),
            vmem(groups * bricks, strip, rank),
            vmem(rank, rank),
            vmem(rank, cols),
            vmem(bricks, strip, cols),
            vmem(rank, cols),
            vmem(rank, 2 * rank),
            dma,
            dma((2, count)),
            dma((2, count)),
            dma((count, groups - 1)),
            dma((count, groups - 1)),
            dma((count, groups - 1)),
            dma((count, groups - 1)),
            dma((2, 2)),
            dma((2, 2)),
        ],
        compiler_params=pltpu.CompilerParams(
            collective_id=0, has_side_effects=True, vmem_limit_bytes=48 * 1024 * 1024
        ),
    )(low_factor, test_matrix)


def solution(mesh):
    return jax.shard_map(
        functools.partial(shards, mesh.shape["grp"], mesh.shape["brick"]),
        mesh=mesh,
        in_specs=(P("brick", None, None, "grp"), P("grp", None)),
        out_specs=(P("brick", None, None, None), P(None, "grp")),
        check_vma=False,
    )
```

```python
import functools

import jax
import jax.numpy as jnp
from jax import lax
from jax.experimental import pallas as pl
from jax.experimental.pallas import tpu as pltpu
from jax.sharding import PartitionSpec as P

DIFF = 0.12
CONV = 0.08
HIGH = lax.Precision.HIGHEST
MESH = pl.DeviceIdType.MESH
BLOCK = 32
GROUP = 8


def dot(left, right, dims):
    return lax.dot_general(
        left, right, (dims, ((), ())), precision=HIGH, preferred_element_type=jnp.float32
    )


def chunk_ends(span_y, slab_x, groups):
    ends = []
    for end in range(3, span_y, 3):
        ends.append((end, end - 1, end - 2))
    ends.append((span_y, span_y, span_y))
    starts = [0] + [end[2] for end in ends]
    if any((b - a) * slab_x % groups for a, b in zip(starts, starts[1:])):
        return [(span_y, span_y, span_y)]
    return ends


def kernel(
    dims, x_hbm, omega_hbm, basis, projected,
    omega, staged, pair_rx, ext, first, grown, part, sketch, group_rx, gram, gram_rx, full, proj, proj_rx, proj_full, both,
    local_sem, out_sem, pair_sem, halo_send, halo_recv, part_send, part_recv, back_send, back_recv, reduce_sem, gather_sem,
):
    groups, bricks, slab, span_y, span_z, cells = dims
    cols, rank = omega.shape
    devices = groups * bricks
    me_g = lax.axis_index("grp")
    me_b = lax.axis_index("brick")
    me = me_g * bricks + me_b
    owners = min(bricks, rank // 8)
    strip = rank // owners
    ends = chunk_ends(span_y, slab, groups)

    def device(g, b):
        return {"grp": g, "brick": b}

    barrier = pltpu.get_barrier_semaphore()

    def greet(d, carry):
        other = lax.rem(me + d, devices)
        g = other // bricks
        pl.semaphore_signal(
            barrier, inc=1, device_id=device(g, other - g * bricks), device_id_type=MESH
        )
        return carry

    lax.fori_loop(1, devices, greet, 0)
    mine = pltpu.make_async_copy(
        x_hbm, ext.at[pl.ds(2, slab), pl.ds(1, span_y)], local_sem.at[0]
    )
    mine.start()
    weights = pltpu.make_async_copy(omega_hbm, omega, local_sem.at[1])
    weights.start()
    layer = (span_z, cols)
    for y in (0, span_y + 1):
        ext[:, y] = jnp.zeros((slab + 4,) + layer, jnp.float32)
        first[:, y] = jnp.zeros((slab + 2,) + layer, jnp.float32)

    @pl.when(me_b == 0)
    def _():
        ext[0:2] = jnp.zeros((2, span_y + 2) + layer, jnp.float32)

    @pl.when(me_b == bricks - 1)
    def _():
        ext[slab + 2 :] = jnp.zeros((2, span_y + 2) + layer, jnp.float32)

    pl.semaphore_wait(barrier, devices - 1)

    def halo(k, up):
        start = 0 if k == 0 else ends[k - 1][0]
        rows = ends[k][0] - start
        side = 0 if up else 1
        return pltpu.make_async_remote_copy(
            src_ref=x_hbm.at[pl.ds(slab - 2 if up else 0, 2), pl.ds(start, rows)],
            dst_ref=ext.at[pl.ds(0 if up else slab + 2, 2), pl.ds(1 + start, rows)],
            send_sem=halo_send.at[side, k],
            recv_sem=halo_recv.at[side, k],
            device_id=device(me_g, me_b + 1 if up else me_b - 1),
            device_id_type=MESH,
        )

    for k in range(len(ends)):
        @pl.when(me_b < bricks - 1)
        def _():
            halo(k, True).start()

        @pl.when(me_b > 0)
        def _():
            halo(k, False).start()

    mine.wait()
    weights.wait()

    def operate(mid, low, high, before, after):
        z = lax.broadcasted_iota(jnp.int32, mid.shape, mid.ndim - 2)
        down = jnp.where(z == 0, 0.0, pltpu.roll(mid, 1, mid.ndim - 2))
        up = jnp.where(z == span_z - 1, 0.0, pltpu.roll(mid, span_z - 1, mid.ndim - 2))
        beside = low + high + before + after + down + up
        return mid - DIFF * beside - CONV * (low - high)

    gate_low = jnp.where(me_b == 0, 0.0, 1.0)
    gate_high = jnp.where(me_b == bricks - 1, 0.0, 1.0)

    def first_row(y, carry):
        for i in range(slab + 2):
            value = operate(
                ext[i + 1, y + 1], ext[i, y + 1], ext[i + 2, y + 1], ext[i + 1, y], ext[i + 1, y + 2]
            )
            if i == 0:
                value = value * gate_low
            if i == slab + 1:
                value = value * gate_high
            first[i, y + 1] = value
        return carry

    def second_row(y, carry):
        values = []
        for i in range(slab):
            value = operate(
                first[i + 1, y + 1], first[i, y + 1], first[i + 2, y + 1],
                first[i + 1, y], first[i + 1, y + 2],
            )
            grown[y * slab + i] = value
            values.append(value)
        rows = jnp.concatenate(values, axis=0)
        terms = dot(rows, omega[...], ((1,), (0,)))
        part[pl.ds(y * slab, slab)] = terms.reshape(slab, span_z, rank)
        return carry

    def piece(k):
        start = 0 if k == 0 else ends[k - 1][2]
        pairs = (ends[k][2] - start) * slab // groups
        return start * slab, pairs

    def part_copy(k, d):
        start, pairs = piece(k)
        other = lax.rem(me_g + d, groups)
        return pltpu.make_async_remote_copy(
            src_ref=part.at[pl.ds(start + other * pairs, pairs)],
            dst_ref=group_rx.at[d - 1, pl.ds(start // groups, pairs)],
            send_sem=part_send.at[k, d - 1],
            recv_sem=part_recv.at[k, d - 1],
            device_id=device(other, me_b),
            device_id_type=MESH,
        )

    def back_copy(k, d):
        start, pairs = piece(k)
        other = lax.rem(me_g + d, groups)
        here = sketch.at[pl.ds(start + me_g * pairs, pairs)]
        return pltpu.make_async_remote_copy(
            src_ref=here,
            dst_ref=here,
            send_sem=back_send.at[k, d - 1],
            recv_sem=back_recv.at[k, d - 1],
            device_id=device(other, me_b),
            device_id_type=MESH,
        )

    def own_rows(k):
        start, pairs = piece(k)
        for d in range(1, groups):
            part_copy(k, d).wait_recv()

        def body(i, carry):
            at = start + me_g * pairs + i
            total = part[at]
            for d in range(groups - 1):
                total = total + group_rx[d, start // groups + i]
            sketch[at] = total
            return carry

        lax.fori_loop(0, pairs, body, 0)
        value = sketch[pl.ds(start + me_g * pairs, pairs)].reshape(pairs * span_z, rank)
        term = dot(value, value, ((0,), (0,)))
        if k == 0:
            gram[...] = term
        else:
            gram[...] += term

    for k, (end, end_first, end_second) in enumerate(ends):
        @pl.when(me_b > 0)
        def _():
            halo(k, True).wait_recv()

        @pl.when(me_b < bricks - 1)
        def _():
            halo(k, False).wait_recv()

        begin_first, begin_second = (0, 0) if k == 0 else ends[k - 1][1:]
        lax.fori_loop(begin_first, end_first, first_row, 0)
        lax.fori_loop(begin_second, end_second, second_row, 0)
        for d in range(1, groups):
            part_copy(k, d).start()
        if k > 0:
            own_rows(k - 1)
    own_rows(len(ends) - 1)

    half = bricks // 2
    side = lax.rem(me_b, 2)

    def strip_at(o):
        q = lax.rem(o, 2) * (owners // 2) + o // 2
        return pl.ds(pl.multiple_of(q * strip, 8), strip)

    def half_at(c):
        return pl.ds(pl.multiple_of(c * (rank // 2), 8), rank // 2)

    pair = pltpu.make_async_remote_copy(
        src_ref=gram.at[half_at(1 - side)],
        dst_ref=pair_rx,
        send_sem=pair_sem.at[0],
        recv_sem=pair_sem.at[1],
        device_id=device(me_g, me_b + 1 - 2 * side),
        device_id_type=MESH,
    )

    def target(d, paired):
        if not paired:
            return me_g, lax.rem(me_b + d, bricks)
        other = lax.rem(me_g * half + me_b // 2 + d, groups * half)
        g = other // half
        return g, (other - g * half) * 2 + side

    def to_owner(source, sink, sem, d, paired, slot):
        g, o = target(d, paired)
        return pltpu.make_async_remote_copy(
            src_ref=source.at[strip_at(o)],
            dst_ref=sink.at[slot],
            send_sem=reduce_sem.at[sem, 0],
            recv_sem=reduce_sem.at[sem, 1],
            device_id=device(g, o),
            device_id_type=MESH,
        )

    def guarded(o, action):
        if owners == bricks:
            action()
        else:
            pl.when(o < owners)(action)

    def scatter_start(source, sink, sem, paired, slot):
        def body(d, carry):
            def send():
                to_owner(source, sink, sem, d, paired, slot).start()

            guarded(target(d, paired)[1], send)
            return carry

        lax.fori_loop(1, groups * half if paired else bricks, body, 0)

        def keep():
            sink[slot] = source[strip_at(me_b)]

        guarded(me_b, keep)

    def bytes_wait(ref, sem):
        pltpu.make_async_copy(ref, ref, sem).wait()

    def scatter_finish(source, sink, sem, paired, result):
        count = groups * half if paired else bricks

        def receive():
            bytes_wait(sink.at[pl.ds(0, count - 1)], reduce_sem.at[sem, 1])

            def add(i, total):
                return total + sink[i]

            result[strip_at(me_b)] = lax.fori_loop(1, count, add, sink[0])

        guarded(me_b, receive)
        copies = groups * owners // 2 if paired else owners
        if owners == bricks:
            bytes_wait(sink.at[pl.ds(0, copies - 1)], reduce_sem.at[sem, 0])
        else:
            @pl.when(me_b < owners)
            def _():
                bytes_wait(sink.at[pl.ds(0, copies - 1)], reduce_sem.at[sem, 0])

            @pl.when(me_b >= owners)
            def _():
                bytes_wait(sink.at[pl.ds(0, copies)], reduce_sem.at[sem, 0])

    def gather_start(result, sem):
        def body(d, carry):
            here = result.at[strip_at(me_b)]
            pltpu.make_async_remote_copy(
                src_ref=here,
                dst_ref=here,
                send_sem=gather_sem.at[sem, 0],
                recv_sem=gather_sem.at[sem, 1],
                device_id=device(me_g, lax.rem(me_b + d, bricks)),
                device_id_type=MESH,
            ).start()
            return carry

        def send():
            lax.fori_loop(1, bricks, body, 0)

        guarded(me_b, send)

    def gather_finish(result, sem, sink):
        rows = strip * (owners - 1)
        if owners == bricks:
            bytes_wait(result.at[pl.ds(0, rows)], gather_sem.at[sem, 1])
            bytes_wait(result.at[pl.ds(0, rows)], gather_sem.at[sem, 0])
        else:
            @pl.when(me_b < owners)
            def _():
                bytes_wait(result.at[pl.ds(0, rows)], gather_sem.at[sem, 1])
                bytes_wait(sink.at[pl.ds(0, bricks - 1)], gather_sem.at[sem, 0])

            @pl.when(me_b >= owners)
            def _():
                bytes_wait(result.at[...], gather_sem.at[sem, 1])

    pair.start()

    def project_piece(k, owner):
        start, pairs = piece(k)
        at = pl.ds(start + owner * pairs, pairs)
        left = sketch[at].reshape(pairs * span_z, rank)
        right = grown[at].reshape(pairs * span_z, cols)
        proj[...] += dot(left, right, ((0,), (0,)))

    pair.wait_recv()
    gram[half_at(side)] += pair_rx[...]
    scatter_start(gram, gram_rx, 0, True, me_g * half + me_b // 2)
    for k in range(len(ends)):
        for d in range(1, groups):
            back_copy(k, d).start()
    proj[...] = jnp.zeros_like(proj)
    for k in range(len(ends)):
        project_piece(k, me_g)
    scatter_finish(gram, gram_rx, 0, True, full)
    gather_start(full, 0)
    gather_finish(full, 0, proj_rx)

    both[:, 0:rank] = full[...]
    row = lax.broadcasted_iota(jnp.int32, (rank, rank), 0)
    col = lax.broadcasted_iota(jnp.int32, (rank, rank), 1)
    both[:, rank:] = jnp.where(row == col, 1.0, 0.0)

    def project(k):
        for d in range(1, groups):
            back_copy(k, d).wait_recv()
            project_piece(k, lax.rem(me_g + d, groups))

    def project_gather():
        scatter_finish(proj, proj_rx, 1, False, proj_full)
        gather_start(proj_full, 1)

    blocks = rank // BLOCK
    last = len(ends) - 1
    hook = blocks // 2 + 1
    for block in range(blocks):
        if block == hook:
            for k in range(last + 1):
                project(k)
            scatter_start(proj, proj_rx, 1, False, me_b)
        at = block * BLOCK
        panel = both[at : at + BLOCK, :]
        row = lax.broadcasted_iota(jnp.int32, (BLOCK, 128), 0)
        for base in range(0, BLOCK, GROUP):
            columns = [
                jnp.broadcast_to(panel[:, at + j : at + j + 1], (BLOCK, 128))
                for j in range(base, base + GROUP)
            ]
            for t in range(GROUP):
                j = base + t
                over = 1.0 / columns[t][j : j + 1, :]
                factor = jnp.where(row > j, columns[t], 0.0)
                for u in range(t + 1, GROUP):
                    columns[u] = columns[u] - factor * (columns[u][j : j + 1, :] * over)
                parts = [
                    panel[:, w : w + 128] - factor * (panel[j : j + 1, w : w + 128] * over)
                    for w in range(0, 2 * rank, 128)
                ]
                panel = jnp.concatenate(parts, axis=1)
        lane = lax.broadcasted_iota(jnp.int32, panel.shape, 1)
        full_row = lax.broadcasted_iota(jnp.int32, panel.shape, 0)
        diagonal = jnp.sum(
            jnp.where(lane == full_row + at, panel, 0.0), axis=1, keepdims=True
        )
        panel = panel * lax.rsqrt(diagonal)
        both[at : at + BLOCK, :] = panel
        done = at + BLOCK
        if done < rank:
            floor = done // 128 * 128
            reach = rank + -(-done // 128) * 128
            below = dot(panel[:, floor:rank], panel[:, floor:reach], ((0,), (0,)))
            both[done:, floor:reach] = both[done:, floor:reach] - below[done - floor :, :]

    project_gather()
    inverse = both[:, rank:]
    scaled_inverse = inverse.T * jnp.sqrt(jnp.float32(cells))
    both[:, 0:rank] = scaled_inverse

    @pl.loop(0, span_y)
    def _(y):
        left = sketch[pl.ds(y * slab, slab)].reshape(slab * span_z, rank)
        value = dot(left, both[:, 0:rank], ((1,), (0,)))
        staged[:, y] = value.reshape(slab, span_z, rank)
        pltpu.make_async_copy(staged.at[:, pl.ds(y, 1)], basis.at[:, pl.ds(y, 1)], out_sem).start()

    gather_finish(proj_full, 1, proj_rx)
    projected[...] = dot(both[:, rank:], proj_full[...], ((1,), (0,)))
    pltpu.make_async_copy(staged, basis, out_sem).wait()
    pair.wait_send()

    for k in range(len(ends)):
        @pl.when(me_b < bricks - 1)
        def _():
            halo(k, True).wait_send()

        @pl.when(me_b > 0)
        def _():
            halo(k, False).wait_send()

        for d in range(1, groups):
            part_copy(k, d).wait_send()
            back_copy(k, d).wait_send()


def shards(groups, bricks, low_factor, test_matrix):
    slab, span_y, span_z, cols = low_factor.shape
    rank = test_matrix.shape[1]
    pairs = slab * span_y
    cells = bricks * pairs * span_z
    owners = min(bricks, rank // 8)
    strip = rank // owners
    count = len(chunk_ends(span_y, slab, groups))
    vmem = lambda *shape: pltpu.VMEM(shape, jnp.float32)
    dma = pltpu.SemaphoreType.DMA
    return pl.pallas_call(
        functools.partial(kernel, (groups, bricks, slab, span_y, span_z, cells)),
        out_shape=(
            jax.ShapeDtypeStruct((slab, span_y, span_z, rank), jnp.float32),
            jax.ShapeDtypeStruct((rank, cols), jnp.float32),
        ),
        in_specs=[pl.BlockSpec(memory_space=pltpu.HBM)] * 2,
        out_specs=[pl.BlockSpec(memory_space=pltpu.HBM), pl.BlockSpec(memory_space=pltpu.VMEM)],
        scratch_shapes=[
            vmem(cols, rank),
            vmem(slab, span_y, span_z, rank),
            vmem(rank // 2, rank),
            vmem(slab + 4, span_y + 2, span_z, cols),
            vmem(slab + 2, span_y + 2, span_z, cols),
            vmem(pairs, span_z, cols),
            vmem(pairs, span_z, rank),
            vmem(pairs, span_z, rank),
            vmem(groups - 1, pairs // groups, span_z, rank),
            vmem(rank, rank),
            vmem(groups * bricks // 2, strip, rank),
            vmem(rank, rank),
            vmem(rank, cols),
            vmem(bricks, strip, cols),
            vmem(rank, cols),
            vmem(rank, 2 * rank),
            dma((2,)),
            dma,
            dma((2,)),
            dma((2, count)),
            dma((2, count)),
            dma((count, groups - 1)),
            dma((count, groups - 1)),
            dma((count, groups - 1)),
            dma((count, groups - 1)),
            dma((2, 2)),
            dma((2, 2)),
        ],
        compiler_params=pltpu.CompilerParams(
            collective_id=0, has_side_effects=True, vmem_limit_bytes=48 * 1024 * 1024
        ),
    )(low_factor, test_matrix)


def solution(mesh):
    return jax.shard_map(
        functools.partial(shards, mesh.shape["grp"], mesh.shape["brick"]),
        mesh=mesh,
        in_specs=(P("brick", None, None, "grp"), P("grp", None)),
        out_specs=(P("brick", None, None, None), P(None, "grp")),
        check_vma=False,
    )
```
